512 devices in a mesh: segment: 64 (over z, y_lo, core), rows: 8 (over x, y_hi).
Axes of the slice: x: 4, y: 4 (y_hi: 2, y_lo: 2; y = y_hi * 2 + y_lo), z: 16, core: 2. Of those that a mesh axis runs over, the one named last changes fastest.
Arguments:
- encoder_weight: bfloat16 [64, 3, 3, 384, 384], P('segment', None, None, 'rows'), may hold values from -0.109375 to 0.109375
- encoder_bias: float32 [64, 384], P('segment'), may hold values from -3 to 3
- decoder_weight: bfloat16 [64, 3, 3, 768, 384], P('segment', None, None, 'rows'), may hold values from -0.078125 to 0.078125
- decoder_bias: float32 [64, 384], P('segment'), may hold values from -3 to 3
- encoder_inputs: bfloat16 [64, 1, 24, 64, 384], P('segment', None, 'rows'), may hold values from -6 to 6
- decoder_inputs: bfloat16 [64, 1, 24, 64, 384], P('segment', None, 'rows'), may hold values from -6 to 6
- arrivals: bfloat16 [3, 1, 24, 64, 384], P(None, None, 'rows'), may hold values from -6 to 6
- skip_buffer: bfloat16 [64, 4, 1, 24, 64, 384], P('segment', None, None, 'rows'), may hold values from -6 to 6
Outputs:
- encoder_results: bfloat16 [64, 4, 1, 24, 64, 384], P('segment', None, None, 'rows')
- decoder_results: bfloat16 [64, 4, 1, 24, 64, 384], P('segment', None, None, 'rows')
The draws below stay inside these ranges and needn't reach their ends.
All inputs are finite; a program needn't handle non-finite values.
Results may differ from the reference program's by a relative error of at most 0.0036.
Values may be sent and summed in bfloat16 or wider, within the bound.
No kernel may reach another device: no remote copies, remote signals or barrier semaphores. Data moves between devices by JAX's collectives and lax.ppermute only.
A program may use at most 64 MiB of HBM per device.

```python
import jax
import jax.numpy as jnp
from jax import lax

C = 384
W = 64
MB = 1
TICKS = 4
H = 24
SEGMENTS = 64


def steps_of(own_key, shape, split, low, top_value):
    level, own = 1.0, jax.random.fold_in(own_key, 6)
    for dim, blocks in split:
        heights = jnp.exp(jax.random.uniform(jax.random.fold_in(own, dim), (blocks,), jnp.float32, low / len(split), top_value / len(split)))
        level = level * jnp.repeat(heights, shape[dim] // blocks).reshape([-1 if axis == dim else 1 for axis in range(len(shape))])
    return level


def bell_draw(stream_key, shape, spread, bound, split=(), kind=jnp.bfloat16):
    array = jax.random.normal(stream_key, shape, jnp.float32) * spread
    if len(split) > 0:
        array = steps_of(stream_key, shape, split, -0.22, 0.18) * array
    return jnp.clip(array, min=-bound, max=bound).astype(kind)


def setup_inputs(seed: int = 0) -> dict:
    arg_keys = jax.random.split(jax.random.key(seed), 9)
    encoder_weight = bell_draw(arg_keys[0], (SEGMENTS, 3, 3, C, C), (9 * C) ** -0.5, 0.109375, ((0, 64), (3, 8)))
    encoder_bias = bell_draw(arg_keys[1], (SEGMENTS, C), 0.5, 3.0, ((0, 64),), jnp.float32)
    decoder_weight = bell_draw(arg_keys[2], (SEGMENTS, 3, 3, 2 * C, C), (18 * C) ** -0.5, 0.078125, ((0, 64), (3, 8)))
    decoder_bias = bell_draw(arg_keys[3], (SEGMENTS, C), 0.5, 3.0, ((0, 64),), jnp.float32)
    encoder_inputs = bell_draw(arg_keys[4], (SEGMENTS, MB, H, W, C), 1.0, 6.0, ((0, 64), (2, 8)))
    decoder_inputs = bell_draw(arg_keys[5], (SEGMENTS, MB, H, W, C), 1.0, 6.0, ((0, 64), (2, 8)))
    arrivals = bell_draw(arg_keys[6], (TICKS - 1, MB, H, W, C), 1.0, 6.0, ((2, 8),))
    skip_buffer = bell_draw(arg_keys[7], (SEGMENTS, TICKS, MB, H, W, C), 1.0, 6.0, ((0, 64), (3, 8)))
    return {"encoder_weight": encoder_weight, "encoder_bias": encoder_bias, "decoder_weight": decoder_weight, "decoder_bias": decoder_bias, "encoder_inputs": encoder_inputs, "decoder_inputs": decoder_inputs, "arrivals": arrivals, "skip_buffer": skip_buffer}


NUMBERS = ("NHWC", "HWIO", "NHWC")


def segment_layer(source, kernel, offset):
    result = lax.conv_general_dilated(source.astype(jnp.float32), kernel.astype(jnp.float32), (1, 1), ((1, 1), (1, 1)), dimension_numbers=NUMBERS, precision=lax.Precision.HIGHEST)
    return jax.nn.silu(result + offset).astype(jnp.bfloat16)


def reference(encoder_weight, encoder_bias, decoder_weight, decoder_bias, encoder_inputs, decoder_inputs, arrivals, skip_buffer):
    layered = jax.vmap(segment_layer)
    skip_lag = 2 * (SEGMENTS - jnp.arange(SEGMENTS, dtype=jnp.int32)) - 1
    encoder_now = encoder_inputs
    decoder_now = decoder_inputs
    encoder_made = []
    decoder_made = []
    for period in range(TICKS):
        skip_now = skip_buffer[:, period]
        for earlier in range(period):
            chosen = (skip_lag == period - earlier)[:, None, None, None, None]
            skip_now = jnp.where(chosen, encoder_made[earlier], skip_now)
        encoder_result = layered(encoder_now, encoder_weight, encoder_bias)
        decoder_result = layered(jnp.concatenate([decoder_now, skip_now], axis=4), decoder_weight, decoder_bias)
        encoder_made.append(encoder_result)
        decoder_made.append(decoder_result)
        if period + 1 < TICKS:
            encoder_now = jnp.concatenate([arrivals[period][None], encoder_result[:-1]], axis=0)
            decoder_now = jnp.concatenate([decoder_result[1:], encoder_result[-1:]], axis=0)
    return jnp.stack(encoder_made, axis=1), jnp.stack(decoder_made, axis=1)
```

```python
import jax
import jax.numpy as jnp
from jax import lax
from jax.experimental import pallas as pl
from jax.experimental.pallas import tpu as pltpu
from jax.sharding import PartitionSpec as P


AXES = ("segment", "rows")
BF = jnp.bfloat16
F32 = jnp.float32
TAPS = 9
LIMIT = 24 * 2**20


def call(arrays, outs, body, scratch=(), flops=0, where=()):
    names = list(arrays)
    arrays = {
        n: pltpu.with_memory_space_constraint(a, pltpu.HBM) if dict(where).get(n) == "hbm" else a
        for n, a in arrays.items()
    }

    def kernel(*refs):
        ins = dict(zip(names, refs))
        rest = refs[len(names) :]
        body(ins, rest[: len(outs)], rest[len(outs) :])

    spaces = {None: pltpu.VMEM, "any": pl.ANY, "hbm": pltpu.HBM}
    vmem = pl.BlockSpec(memory_space=pltpu.VMEM)
    shapes = [jax.ShapeDtypeStruct(s, d) for s, d in outs]
    nbytes = sum(a.size * a.dtype.itemsize for a in arrays.values())
    return pl.pallas_call(
        kernel,
        out_shape=shapes,
        in_specs=[pl.BlockSpec(memory_space=spaces[dict(where).get(n)]) for n in names],
        out_specs=[vmem] * len(outs),
        scratch_shapes=list(scratch),
        compiler_params=pltpu.CompilerParams(vmem_limit_bytes=LIMIT),
        cost_estimate=pl.CostEstimate(flops=flops, bytes_accessed=nbytes, transcendentals=0),
    )(*arrays.values())


def put(ref, views):
    at = 0
    for view in views:
        if isinstance(view, int):
            at += view
            continue
        if len(view.shape) == 2:
            view = view[...].reshape((-1,) + ref.shape[1:])
        ref[at : at + view.shape[0]] = view[...]
        at += view.shape[0]


def fill(x_ref, cases, own, total):
    for when, views in cases:
        pl.when(when)(lambda views=views: put(x_ref, views))
    count = x_ref.shape[0]
    rim = (count - own) // 2
    first = lax.axis_index("rows") * own - rim
    for i in list(range(rim)) + list(range(count - rim, count)):

        @pl.when((first + i < 0) | (first + i >= total))
        def _():
            x_ref[i] = jnp.zeros(x_ref.shape[1:], x_ref.dtype)


def patches(x_ref):
    rows, (width, channels) = x_ref.shape[0] - 2, x_ref.shape[1:]
    parts = [x_ref[t : t + rows].reshape(rows * width, channels) for t in range(3)]
    return jnp.concatenate(parts, axis=1)


def products(left, w_refs, y_ref):
    for column in range(3):
        right = jnp.concatenate([w[3 * t + column] for w in w_refs for t in range(3)], axis=0)
        y_ref[column] = jnp.dot(left, right, preferred_element_type=F32)


def combine(y_ref, row, width):
    span = pl.ds(row * width, width)
    place = lax.broadcasted_iota(jnp.int32, (width, y_ref.shape[2]), 0)
    before = jnp.where(place == 0, 0.0, pltpu.roll(y_ref[0, span], 1, 0))
    after = jnp.where(place == width - 1, 0.0, pltpu.roll(y_ref[2, span], width - 1, 0))
    return y_ref[1, span] + before + after


def finish(x_refs, w_refs, y_ref, bias_ref, ready, acc_ref, store):
    rows, width = x_refs[0].shape[0] - 2, x_refs[0].shape[1]
    left = [patches(x) for x in x_refs]
    left = left[0] if len(left) == 1 else jnp.concatenate(left, axis=1)
    products(left, w_refs, y_ref)
    ready.wait()
    bias = bias_ref[...]
    for row in range(rows):
        v = combine(y_ref, row, width) + bias
        if acc_ref is not None:
            v = v + acc_ref[row]
        store(row, (v / (1.0 + jnp.exp(-v))).astype(BF))


def sources(ring):
    block = lax.axis_index("rows")
    near = [block, lax.rem(block + ring - 2, ring), lax.rem(block + 2, ring)]
    far = lax.rem(block + 4, ring)
    swap = lambda r: r + 1 - 2 * lax.rem(r, 2)
    return near + [swap(block), far, swap(near[1]), swap(near[2]), swap(far)]


def shards(
    encoder_weight,
    encoder_bias,
    decoder_weight,
    decoder_bias,
    encoder_inputs,
    decoder_inputs,
    arrivals,
    skip_buffer,
):
    segments = lax.axis_size("segment")
    ring = lax.axis_size("rows")
    own, width, channels = encoder_inputs.shape[2:]
    outs = encoder_weight.shape[4]
    total = own * ring

    def pairs(move):
        found = []
        for s in range(segments):
            for r in range(ring):
                ts, tr = move(s, r)
                if 0 <= ts < segments and 0 <= tr < ring:
                    found.append((s * ring + r, ts * ring + tr))
        return found

    ahead = pairs(lambda s, r: (s, (r + 2) % ring))
    behind = pairs(lambda s, r: (s, (r - 2) % ring))
    opposite = pairs(lambda s, r: (s, (r + 4) % ring))
    across = pairs(lambda s, r: (s, r ^ 1))
    step = lambda r: r + 1 if r % 2 else r - 1
    cross = pairs(lambda s, r: (s, step(r)))
    first_across = pairs(lambda s, r: (s, r ^ 1 if s == 0 else -1))
    first_cross = pairs(lambda s, r: (s, step(r) if s == 0 else -1))
    up = pairs(lambda s, r: (s + 1, r))
    down = pairs(lambda s, r: (s - 1, r))
    down_after = pairs(lambda s, r: (s - 1, r + 1))
    down_before = pairs(lambda s, r: (s - 1, r - 1))

    def send(value, route):
        return lax.ppermute(value, AXES, route)

    enc_in = encoder_inputs[0, 0]
    dec_in = decoder_inputs[0, 0]
    skip = skip_buffer[0, :, 0]
    arr = arrivals[:, 0]
    image = (width, channels)

    e_own = encoder_weight.reshape(TAPS, -1, outs)
    d_own = decoder_weight.reshape(TAPS, -1, outs)
    ke, kd = e_own.shape[1], d_own.shape[1]

    ne = TAPS * ke

    ne = TAPS * ke
    extra = -(-width // ke)

    depth = [3, 2, 2, 1, 2, 1]
    arr_depth = [3, 2, 1]
    starts = [sum(depth[:i]) for i in range(len(depth) + 1)]
    arr_starts = [sum(arr_depth[:i]) for i in range(len(arr_depth) + 1)]


    chunks = [(n, n * ke, min(width, (n + 1) * ke)) for n in range(extra)]

    def pack(ins, out, scratch):
        sems = scratch[0]
        even = lax.rem(lax.axis_index("rows"), 2) == 0
        rows = [ins["enc"], ins["dec"]] + [ins["skip"].at[t] for t in range(4)]
        arrs = [ins["arr"].at[t] for t in range(3)]
        jobs = []
        for first, second, group, sizes in (
            (out[0], out[1], rows, depth),
            (out[2], out[3], arrs, arr_depth),
        ):
            at = 0
            for a, n in zip(group, sizes):
                last, head = a.at[own - n : own], a.at[0:n]
                to = [o.at[at : at + n] for o in (first, second)]
                jobs.append(((last, to[0]), (head, to[0])))
                jobs.append(((head, to[1]), (last, to[1])))
                at += n
        for o, row in ((out[4], own - 1), (out[5], 0)):
            jobs.append(((ins["e"], o.at[:TAPS]),) * 2)
            for n, low, high in chunks:
                jobs.append(((ins["enc"].at[row, low:high], o.at[TAPS + n, 0 : high - low]),) * 2)
        waits = []
        for i, (one, other) in enumerate(jobs):
            one, other = (pltpu.make_async_copy(*c, sems.at[i]) for c in (one, other))
            pl.when(even)(one.start)
            pl.when(~even)(other.start)
            waits.append(one)
        for wait in waits:
            wait.wait()

    count = 2 * (len(depth) + len(arr_depth)) + 2 * (1 + extra)
    sources_in = {"enc": enc_in, "dec": dec_in, "skip": skip, "arr": arr, "e": e_own}
    pay = call(
        sources_in,
        [((starts[-1],) + image, BF)] * 2
        + [((arr_starts[-1],) + image, BF)] * 2
        + [((TAPS + extra, ke, outs), BF)] * 2,
        pack,
        [pltpu.SemaphoreType.DMA((count,))],
        where={n: "hbm" for n in sources_in},
    )

    def join(far):
        def body(ins, out, scratch):
            out[0][:ne] = ins["w"][...].reshape(ne, outs)
            out[0][ne:] = ins["rims"][...].reshape(-1, outs)

        return call({"w": far, "rims": pay[0]}, [((ne + starts[-1] * width, outs), BF)], body)[0]

    def pick(ins, out, scratch):
        even = lax.rem(lax.axis_index("rows"), 2) == 0
        copies = [pltpu.make_async_copy(ins[n], out[0], scratch[0]) for n in ("ahead", "behind")]
        pl.when(even)(copies[0].start)
        pl.when(~even)(copies[1].start)
        copies[0].wait()

    e_pieces = {"p0": pay[4], "p1": send(pay[4], ahead), "p2": send(pay[5], behind)}
    e_pieces["p3"] = send(e_own, across)
    e_pieces["p4"] = send(e_own, opposite)
    e_pieces["p5"] = send(e_pieces["p3"], ahead)
    e_pieces["p6"] = send(e_pieces["p3"], behind)
    e_pieces["p7"] = send(join(e_pieces["p4"]), across)

    d_pieces = {"p0": d_own, "p1": send(d_own, ahead), "p2": send(d_own, behind)}
    d_pieces["p3"] = send(d_own, across)
    picked = call(
        {"ahead": d_pieces["p1"], "behind": d_pieces["p2"]},
        [(d_own.shape, BF)],
        pick,
        [pltpu.SemaphoreType.DMA(())],
        where={"ahead": "any", "behind": "any"},
    )[0]
    forward = pairs(lambda s, r: (s, (r - 2) % ring if r % 2 else (r + 2) % ring))
    d_pieces["p4"] = send(picked, forward)
    d_pieces["p5"] = send(d_pieces["p3"], ahead)
    d_pieces["p6"] = send(d_pieces["p3"], behind)
    d_pieces["p7"] = send(d_pieces["p4"], across)
    rims = {"pair": e_pieces["p7"], "cross": send(pay[1], cross)}
    arr_rims = {"pair": send(pay[2], first_across), "cross": send(pay[3], first_cross)}

    def around(pair, cross_rim, middle, before=0, after=0, also=None):
        even = lax.rem(lax.axis_index("rows"), 2) == 0
        both = lambda c: c if also is None else c & also
        return [
            (both(even), [before, cross_rim, middle, pair, after]),
            (both(~even), [before, pair, middle, cross_rim, after]),
        ]

    def rim_rows(ins, n):
        low, high = starts[n], starts[n + 1]
        pair = ins["pair"] if "pair" in ins else ins["p7"]
        return pair.at[ne + low * width : ne + high * width], ins["cross"].at[low:high]

    def arr_rows(ins, t):
        return [ins[n].at[arr_starts[t] : arr_starts[t + 1]] for n in ("pair", "cross")]

    def begin(jobs, sems, at=0):
        copies = [pltpu.make_async_copy(*job, sems.at[at + i]) for i, job in enumerate(jobs)]
        for copy in copies:
            copy.start()
        return copies

    def moves(piece, k, w_ref, place):
        if len(piece.shape) == 3:
            return [(piece.at[0:TAPS], w_ref.at[:, place])]
        return [(piece.at[t * k : (t + 1) * k], w_ref.at[t, place]) for t in range(TAPS)]

    bias_scratch = [pltpu.VMEM((1, outs), F32), pltpu.SemaphoreType.DMA((1,))]

    def x_scratch(rows):
        return pltpu.VMEM((rows,) + image, BF)

    def y_scratch(rows):
        return pltpu.VMEM((3, rows * width, outs), F32)

    def cost(rows, groups=1):
        return 4 * rows * width * TAPS * groups * channels * outs

    def enc0_body(ins, out, scratch):
        x_ref, y_ref, sems, bias_ref, few = scratch
        w_ref = out[1]
        (bias,) = begin([(ins["bias"], bias_ref)], few)
        jobs = []
        for i, source in enumerate(sources(ring)):
            place = pl.ds(pl.multiple_of(source * ke, ke), ke)
            jobs += moves(ins[f"p{i}"], ke, w_ref, place)
        copies = begin(jobs, sems)
        for n, low, high in chunks:
            x_ref[0, low:high] = ins["p1"][TAPS + n, 0 : high - low]
            x_ref[own + 7, low:high] = ins["p2"][TAPS + n, 0 : high - low]
        fill(x_ref, around(*rim_rows(ins, 0), ins["enc"], 1, 1), own, total)
        for copy in copies:
            copy.wait()

        def store(row, v):
            out[0][row] = v

        finish([x_ref], [w_ref], y_ref, bias_ref, bias, None, store)

    e0, w_enc = call(
        {**e_pieces, "cross": rims["cross"], "enc": enc_in, "bias": encoder_bias},
        [((own + 6,) + image, BF), ((TAPS, ke * ring, outs), BF)],
        enc0_body,
        [x_scratch(own + 8), y_scratch(own + 6), pltpu.SemaphoreType.DMA((7 + TAPS,))]
        + bias_scratch,
        cost(own + 6),
        {"p3": "any", "p4": "any", "p5": "any", "p6": "any", "bias": "hbm"},
    )

    def enc_body(t, ins, out, scratch):
        x_ref, y_ref, bias_ref, few = scratch
        (bias,) = begin([(ins["bias"], bias_ref)], few)
        first = lax.axis_index("segment") == 0
        cases = [(~first, [ins["moved"]])]
        cases += around(*arr_rows(ins, t), ins["arr"].at[t], also=first)
        fill(x_ref, cases, own, total)
        if t < 2:

            def store(row, v):
                out[0][row] = v
        else:
            for n in range(3):
                out[0][n] = ins[f"e{n}"][3 - n : 3 - n + own]

            def store(row, v):
                out[0][3, row] = v

        finish([x_ref], [ins["w"]], y_ref, bias_ref, bias, None, store)

    made = [e0]
    for t in range(3):
        rows = own + 4 - 2 * t
        arrays = {"moved": send(made[t], up), **arr_rims, "arr": arr}
        arrays |= {"w": w_enc, "bias": encoder_bias}
        if t == 2:
            arrays |= {f"e{n}": made[n] for n in range(3)}
        shape = ((rows,) if t < 2 else (4, own)) + image
        made += call(
            arrays,
            [(shape, BF)],
            lambda ins, out, scratch, t=t: enc_body(t, ins, out, scratch),
            [x_scratch(rows + 2), y_scratch(rows)] + bias_scratch,
            cost(rows),
            {"bias": "hbm"},
        )
    enc_all = made.pop()

    def dec0_body(ins, out, scratch):
        x_ref, s_ref, y_ref, sems, bias_ref, few = scratch
        halves = out[1:3]
        (bias,) = begin([(ins["bias"], bias_ref)], few)
        half = ring // 2
        waits = []
        for i, source in enumerate(sources(ring)):
            place = pl.ds(pl.multiple_of(lax.rem(source, half) * kd, kd), kd)
            jobs = [moves(ins[f"p{i}"], kd, w, place)[0] for w in halves]
            copies = [pltpu.make_async_copy(*job, sems.at[i]) for job in jobs]
            pl.when(source < half)(copies[0].start)
            pl.when(source >= half)(copies[1].start)
            waits.append(copies[0])
        fill(x_ref, around(*rim_rows(ins, 1), ins["dec"]), own, total)
        fill(s_ref, around(*rim_rows(ins, 2), ins["skip"].at[0]), own, total)
        for copy in waits:
            copy.wait()

        def store(row, v):
            out[0][row] = v

        finish([x_ref, s_ref], halves, y_ref, bias_ref, bias, None, store)

    w_half = ((TAPS, kd * ring // 2, outs), BF)
    d0, w_dec, w_skip = call(
        {**d_pieces, **rims, "dec": dec_in, "skip": skip, "bias": decoder_bias},
        [((own + 2,) + image, BF), w_half, w_half],
        dec0_body,
        [x_scratch(own + 4)] * 2
        + [y_scratch(own + 2), pltpu.SemaphoreType.DMA((8,))]
        + bias_scratch,
        cost(own + 2, 2),
        {"bias": "hbm"} | {f"p{i}": "any" for i in range(8)},
    )

    handed = {1: ("e0", 2, own + 2), 2: ("e1", 0, own + 4), 3: ("e2", 0, own + 2)}
    results = {f"e{n}": made[n] for n in range(3)}

    def handed_view(ins, t):
        name, at, rows = handed[t]
        return ins[name].at[at : at + rows]

    skip_rows = [own, own + 2, own]

    def skip_body(ins, out, scratch):
        x_refs, y_ref = scratch[:3], scratch[3]
        lag = 2 * (segments - lax.axis_index("segment")) - 1
        for t in range(1, 4):
            cases = [(lag == 1, [handed_view(ins, t)])]
            plain = lag != 1
            if t == 3:
                cases.append((lag == 3, [handed_view(ins, 1)]))
                plain = plain & (lag != 3)
            cases += around(*rim_rows(ins, 2 + t), ins["skip"].at[t], also=plain)
            fill(x_refs[t - 1], cases, own, total)
        left = jnp.concatenate([patches(x) for x in x_refs], axis=0)
        products(left, [ins["w"]], y_ref)
        at = 0
        for o in out:
            for row in range(o.shape[0]):
                o[row] = combine(y_ref, at, width)
                at += 1

    acc = call(
        {**rims, **results, "skip": skip, "w": w_skip},
        [((r,) + image[:1] + (outs,), F32) for r in skip_rows],
        skip_body,
        [x_scratch(r + 2) for r in skip_rows] + [y_scratch(sum(skip_rows))],
        cost(sum(skip_rows)),
    )

    def dec_body(t, moved, ins, out, scratch):
        x_ref, y_ref, bias_ref, few = scratch
        (bias,) = begin([(ins["bias"], bias_ref)], few)
        last = lax.axis_index("segment") == segments - 1
        cases = [(~last, [ins[m] for m in moved]), (last, [handed_view(ins, t)])]
        fill(x_ref, cases, own, total)
        if t == 3:
            out[0][0] = ins["d0"][1 : 1 + own]
            out[0][1] = ins["d1"][...]
            out[0][2] = ins["d2"][1 : 1 + own]

        def store(row, v):
            if t == 3:
                out[0][3, row] = v
            else:
                out[0][row] = v
            if t == 1 and row < 2:
                out[1][row] = v
            if t == 1 and row >= own - 2:
                out[2][row - own + 2] = v

        finish([x_ref], [ins["w"]], y_ref, bias_ref, bias, ins["acc"], store)

    def dec(t, rows, moved, shapes, more=()):
        arrays = dict(moved)
        name = handed[t][0]
        arrays |= {name: results[name], "w": w_dec, "bias": decoder_bias, "acc": acc[t - 1]}
        arrays |= dict(more)
        return call(
            arrays,
            [(s + image, BF) for s in shapes],
            lambda ins, out, scratch: dec_body(t, list(moved), ins, out, scratch),
            [x_scratch(rows + 2), y_scratch(rows)] + bias_scratch,
            cost(rows),
            {"bias": "hbm"},
        )

    d1, d1_head, d1_last = dec(1, own, {"m": send(d0, down)}, [(own,), (2,), (2,)])
    moved = {
        "before": send(d1_last, down_after),
        "m": send(d1, down),
        "after": send(d1_head, down_before),
    }
    (d2,) = dec(2, own + 2, moved, [(own + 2,)])
    (dec_all,) = dec(3, own, {"m": send(d2, down)}, [(4, own)], {"d0": d0, "d1": d1, "d2": d2})
    shape = (1, 4, 1, own, width, outs)
    return enc_all.reshape(shape), dec_all.reshape(shape)


def solution(mesh):
    return jax.shard_map(
        shards,
        mesh=mesh,
        in_specs=(
            P("segment", None, None, "rows", None),
            P("segment", None),
            P("segment", None, None, "rows", None),
            P("segment", None),
            P("segment", None, "rows", None, None),
            P("segment", None, "rows", None, None),
            P(None, None, "rows", None, None),
            P("segment", None, None, "rows", None, None),
        ),
        out_specs=(
            P("segment", None, None, "rows", None, None),
            P("segment", None, None, "rows", None, None),
        ),
        check_vma=False,
    )
```

```python
import jax
import jax.numpy as jnp
from jax import lax
from jax.experimental import pallas as pl
from jax.experimental.pallas import tpu as pltpu
from jax.sharding import PartitionSpec as P


AXES = ("segment", "rows")
BF = jnp.bfloat16
F32 = jnp.float32
TAPS = 9
LIMIT = 24 * 2**20


def call(arrays, outs, body, scratch=(), flops=0, where=()):
    names = list(arrays)
    arrays = {
        n: pltpu.with_memory_space_constraint(a, pltpu.HBM) if dict(where).get(n) == "hbm" else a
        for n, a in arrays.items()
    }

    def kernel(*refs):
        ins = dict(zip(names, refs))
        rest = refs[len(names) :]
        body(ins, rest[: len(outs)], rest[len(outs) :])

    spaces = {None: pltpu.VMEM, "any": pl.ANY, "hbm": pltpu.HBM}
    vmem = pl.BlockSpec(memory_space=pltpu.VMEM)
    shapes = [jax.ShapeDtypeStruct(s, d) for s, d in outs]
    nbytes = sum(a.size * a.dtype.itemsize for a in arrays.values())
    return pl.pallas_call(
        kernel,
        out_shape=shapes,
        in_specs=[pl.BlockSpec(memory_space=spaces[dict(where).get(n)]) for n in names],
        out_specs=[vmem] * len(outs),
        scratch_shapes=list(scratch),
        compiler_params=pltpu.CompilerParams(vmem_limit_bytes=LIMIT),
        cost_estimate=pl.CostEstimate(flops=flops, bytes_accessed=nbytes, transcendentals=0),
    )(*arrays.values())


def put(ref, views):
    at = 0
    for view in views:
        if isinstance(view, int):
            at += view
            continue
        if len(view.shape) == 2:
            view = view[...].reshape((-1,) + ref.shape[1:])
        ref[at : at + view.shape[0]] = view[...]
        at += view.shape[0]


def fill(x_ref, cases, own, total):
    for when, views in cases:
        pl.when(when)(lambda views=views: put(x_ref, views))
    count = x_ref.shape[0]
    rim = (count - own) // 2
    first = lax.axis_index("rows") * own - rim
    for i in list(range(rim)) + list(range(count - rim, count)):

        @pl.when((first + i < 0) | (first + i >= total))
        def _():
            x_ref[i] = jnp.zeros(x_ref.shape[1:], x_ref.dtype)


def patches(x_ref):
    rows, (width, channels) = x_ref.shape[0] - 2, x_ref.shape[1:]
    parts = [x_ref[t : t + rows].reshape(rows * width, channels) for t in range(3)]
    return jnp.concatenate(parts, axis=1)


def products(left, w_refs, y_ref):
    for column in range(3):
        right = jnp.concatenate([w[3 * t + column] for w in w_refs for t in range(3)], axis=0)
        y_ref[column] = jnp.dot(left, right, preferred_element_type=F32)


def combine(y_ref, row, width):
    span = pl.ds(row * width, width)
    place = lax.broadcasted_iota(jnp.int32, (width, y_ref.shape[2]), 0)
    before = jnp.where(place == 0, 0.0, pltpu.roll(y_ref[0, span], 1, 0))
    after = jnp.where(place == width - 1, 0.0, pltpu.roll(y_ref[2, span], width - 1, 0))
    return y_ref[1, span] + before + after


def finish(x_refs, w_refs, y_ref, bias_ref, ready, acc_ref, store):
    rows, width = x_refs[0].shape[0] - 2, x_refs[0].shape[1]
    left = [patches(x) for x in x_refs]
    left = left[0] if len(left) == 1 else jnp.concatenate(left, axis=1)
    products(left, w_refs, y_ref)
    ready.wait()
    bias = bias_ref[...]
    for row in range(rows):
        v = combine(y_ref, row, width) + bias
        if acc_ref is not None:
            v = v + acc_ref[row]
        store(row, (v / (1.0 + jnp.exp(-v))).astype(BF))


def sources(ring):
    block = lax.axis_index("rows")
    near = [block, lax.rem(block + ring - 2, ring), lax.rem(block + 2, ring)]
    far = lax.rem(block + 4, ring)
    swap = lambda r: r + 1 - 2 * lax.rem(r, 2)
    return near + [swap(block), far, swap(near[1]), swap(near[2]), swap(far)]


def shards(
    encoder_weight,
    encoder_bias,
    decoder_weight,
    decoder_bias,
    encoder_inputs,
    decoder_inputs,
    arrivals,
    skip_buffer,
):
    segments = lax.axis_size("segment")
    ring = lax.axis_size("rows")
    own, width, channels = encoder_inputs.shape[2:]
    outs = encoder_weight.shape[4]
    total = own * ring

    def pairs(move):
        found = []
        for s in range(segments):
            for r in range(ring):
                ts, tr = move(s, r)
                if 0 <= ts < segments and 0 <= tr < ring:
                    found.append((s * ring + r, ts * ring + tr))
        return found

    ahead = pairs(lambda s, r: (s, (r + 2) % ring))
    behind = pairs(lambda s, r: (s, (r - 2) % ring))
    opposite = pairs(lambda s, r: (s, (r + 4) % ring))
    across = pairs(lambda s, r: (s, r ^ 1))
    step = lambda r: r + 1 if r % 2 else r - 1
    cross = pairs(lambda s, r: (s, step(r)))
    first_across = pairs(lambda s, r: (s, r ^ 1 if s == 0 else -1))
    first_cross = pairs(lambda s, r: (s, step(r) if s == 0 else -1))
    up = pairs(lambda s, r: (s + 1, r))
    down = pairs(lambda s, r: (s - 1, r))
    down_after = pairs(lambda s, r: (s - 1, r + 1))
    down_before = pairs(lambda s, r: (s - 1, r - 1))

    def send(value, route):
        return lax.ppermute(value, AXES, route)

    enc_in = encoder_inputs[0, 0]
    dec_in = decoder_inputs[0, 0]
    skip = skip_buffer[0, :, 0]
    arr = arrivals[:, 0]
    image = (width, channels)

    e_own = encoder_weight.reshape(TAPS, -1, outs)
    d_own = decoder_weight.reshape(TAPS, -1, outs)
    ke, kd = e_own.shape[1], d_own.shape[1]

    ne = TAPS * ke

    ne = TAPS * ke
    extra = -(-width // ke)

    depth = [3, 2, 2, 1, 2, 1]
    arr_depth = [3, 2, 1]
    starts = [sum(depth[:i]) for i in range(len(depth) + 1)]
    arr_starts = [sum(arr_depth[:i]) for i in range(len(arr_depth) + 1)]


    chunks = [(n, n * ke, min(width, (n + 1) * ke)) for n in range(extra)]

    def pack(ins, out, scratch):
        sems = scratch[0]
        even = lax.rem(lax.axis_index("rows"), 2) == 0
        rows = [ins["enc"], ins["dec"]] + [ins["skip"].at[t] for t in range(4)]
        arrs = [ins["arr"].at[t] for t in range(3)]
        jobs = []
        for first, second, group, sizes in (
            (out[0], out[1], rows, depth),
            (out[2], out[3], arrs, arr_depth),
        ):
            at = 0
            for a, n in zip(group, sizes):
                last, head = a.at[own - n : own], a.at[0:n]
                to = [o.at[at : at + n] for o in (first, second)]
                jobs.append(((last, to[0]), (head, to[0])))
                jobs.append(((head, to[1]), (last, to[1])))
                at += n
        for o, row in ((out[4], own - 1), (out[5], 0)):
            jobs.append(((ins["e"], o.at[:TAPS]),) * 2)
            for n, low, high in chunks:
                jobs.append(((ins["enc"].at[row, low:high], o.at[TAPS + n, 0 : high - low]),) * 2)
        waits = []
        for i, (one, other) in enumerate(jobs):
            one, other = (pltpu.make_async_copy(*c, sems.at[i]) for c in (one, other))
            pl.when(even)(one.start)
            pl.when(~even)(other.start)
            waits.append(one)
        for wait in waits:
            wait.wait()

    count = 2 * (len(depth) + len(arr_depth)) + 2 * (1 + extra)
    sources_in = {"enc": enc_in, "dec": dec_in, "skip": skip, "arr": arr, "e": e_own}
    pay = call(
        sources_in,
        [((starts[-1],) + image, BF)] * 2
        + [((arr_starts[-1],) + image, BF)] * 2
        + [((TAPS + extra, ke, outs), BF)] * 2,
        pack,
        [pltpu.SemaphoreType.DMA((count,))],
        where={n: "hbm" for n in sources_in},
    )

    def join(far):
        def body(ins, out, scratch):
            out[0][:ne] = ins["w"][...].reshape(ne, outs)
            out[0][ne:] = ins["rims"][...].reshape(-1, outs)

        return call({"w": far, "rims": pay[0]}, [((ne + starts[-1] * width, outs), BF)], body)[0]

    def pick(ins, out, scratch):
        even = lax.rem(lax.axis_index("rows"), 2) == 0
        copies = [pltpu.make_async_copy(ins[n], out[0], scratch[0]) for n in ("ahead", "behind")]
        pl.when(even)(copies[0].start)
        pl.when(~even)(copies[1].start)
        copies[0].wait()

    e_pieces = {"p0": pay[4], "p1": send(pay[4], ahead), "p2": send(pay[5], behind)}
    e_pieces["p3"] = send(e_own, across)
    e_pieces["p4"] = send(e_own, opposite)
    e_pieces["p5"] = send(e_pieces["p3"], ahead)
    e_pieces["p6"] = send(e_pieces["p3"], behind)
    e_pieces["p7"] = send(join(e_pieces["p4"]), across)

    d_pieces = {"p0": d_own, "p1": send(d_own, ahead), "p2": send(d_own, behind)}
    d_pieces["p3"] = send(d_own, across)
    picked = call(
        {"ahead": d_pieces["p1"], "behind": d_pieces["p2"]},
        [(d_own.shape, BF)],
        pick,
        [pltpu.SemaphoreType.DMA(())],
        where={"ahead": "any", "behind": "any"},
    )[0]
    forward = pairs(lambda s, r: (s, (r - 2) % ring if r % 2 else (r + 2) % ring))
    d_pieces["p4"] = send(picked, forward)
    d_pieces["p5"] = send(d_pieces["p3"], ahead)
    d_pieces["p6"] = send(d_pieces["p3"], behind)
    d_pieces["p7"] = send(d_pieces["p4"], across)
    rims = {"pair": e_pieces["p7"], "cross": send(pay[1], cross)}
    arr_rims = {"pair": send(pay[2], first_across), "cross": send(pay[3], first_cross)}

    def around(pair, cross_rim, middle, before=0, after=0, also=None):
        even = lax.rem(lax.axis_index("rows"), 2) == 0
        both = lambda c: c if also is None else c & also
        return [
            (both(even), [before, cross_rim, middle, pair, after]),
            (both(~even), [before, pair, middle, cross_rim, after]),
        ]

    def rim_rows(ins, n):
        low, high = starts[n], starts[n + 1]
        pair = ins["pair"] if "pair" in ins else ins["p7"]
        return pair.at[ne + low * width : ne + high * width], ins["cross"].at[low:high]

    def arr_rows(ins, t):
        return [ins[n].at[arr_starts[t] : arr_starts[t + 1]] for n in ("pair", "cross")]

    def begin(jobs, sems, at=0):
        copies = [pltpu.make_async_copy(*job, sems.at[at + i]) for i, job in enumerate(jobs)]
        for copy in copies:
            copy.start()
        return copies

    def moves(piece, k, w_ref, place):
        if len(piece.shape) == 3:
            return [(piece.at[0:TAPS], w_ref.at[:, place])]
        return [(piece.at[t * k : (t + 1) * k], w_ref.at[t, place]) for t in range(TAPS)]

    bias_scratch = [pltpu.VMEM((1, outs), F32), pltpu.SemaphoreType.DMA((1,))]

    def x_scratch(rows):
        return pltpu.VMEM((rows,) + image, BF)

    def y_scratch(rows):
        return pltpu.VMEM((3, rows * width, outs), F32)

    def cost(rows, groups=1):
        return 4 * rows * width * TAPS * groups * channels * outs

    def enc0_body(ins, out, scratch):
        x_ref, y_ref, sems, bias_ref, few = scratch
        w_ref = out[1]
        (bias,) = begin([(ins["bias"], bias_ref)], few)
        jobs = []
        for i, source in enumerate(sources(ring)):
            place = pl.ds(pl.multiple_of(source * ke, ke), ke)
            jobs += moves(ins[f"p{i}"], ke, w_ref, place)
        copies = begin(jobs, sems)
        for n, low, high in chunks:
            x_ref[0, low:high] = ins["p1"][TAPS + n, 0 : high - low]
            x_ref[own + 7, low:high] = ins["p2"][TAPS + n, 0 : high - low]
        fill(x_ref, around(*rim_rows(ins, 0), ins["enc"], 1, 1), own, total)
        for copy in copies:
            copy.wait()

        def store(row, v):
            out[0][row] = v

        finish([x_ref], [w_ref], y_ref, bias_ref, bias, None, store)

    e0, w_enc = call(
        {**e_pieces, "cross": rims["cross"], "enc": enc_in, "bias": encoder_bias},
        [((own + 6,) + image, BF), ((TAPS, ke * ring, outs), BF)],
        enc0_body,
        [x_scratch(own + 8), y_scratch(own + 6), pltpu.SemaphoreType.DMA((7 + TAPS,))]
        + bias_scratch,
        cost(own + 6),
        {"p3": "any", "p4": "any", "p5": "any", "p6": "any", "bias": "hbm"},
    )

    def enc_body(t, ins, out, scratch):
        x_ref, y_ref, bias_ref, few = scratch
        (bias,) = begin([(ins["bias"], bias_ref)], few)
        first = lax.axis_index("segment") == 0
        cases = [(~first, [ins["moved"]])]
        cases += around(*arr_rows(ins, t), ins["arr"].at[t], also=first)
        fill(x_ref, cases, own, total)
        if t < 2:

            def store(row, v):
                out[0][row] = v
        else:
            for n in range(3):
                out[0][n] = ins[f"e{n}"][3 - n : 3 - n + own]

            def store(row, v):
                out[0][3, row] = v

        finish([x_ref], [ins["w"]], y_ref, bias_ref, bias, None, store)

    made = [e0]
    for t in range(3):
        rows = own + 4 - 2 * t
        arrays = {"moved": send(made[t], up), **arr_rims, "arr": arr}
        arrays |= {"w": w_enc, "bias": encoder_bias}
        if t == 2:
            arrays |= {f"e{n}": made[n] for n in range(3)}
        shape = ((rows,) if t < 2 else (4, own)) + image
        made += call(
            arrays,
            [(shape, BF)],
            lambda ins, out, scratch, t=t: enc_body(t, ins, out, scratch),
            [x_scratch(rows + 2), y_scratch(rows)] + bias_scratch,
            cost(rows),
            {"bias": "hbm"},
        )
    enc_all = made.pop()

    def dec0_body(ins, out, scratch):
        x_ref, s_ref, y_ref, sems, bias_ref, few = scratch
        halves = out[1:3]
        (bias,) = begin([(ins["bias"], bias_ref)], few)
        half = ring // 2
        waits = []
        for i, source in enumerate(sources(ring)):
            place = pl.ds(pl.multiple_of(lax.rem(source, half) * kd, kd), kd)
            jobs = [moves(ins[f"p{i}"], kd, w, place)[0] for w in halves]
            copies = [pltpu.make_async_copy(*job, sems.at[i]) for job in jobs]
            pl.when(source < half)(copies[0].start)
            pl.when(source >= half)(copies[1].start)
            waits.append(copies[0])
        fill(x_ref, around(*rim_rows(ins, 1), ins["dec"]), own, total)
        fill(s_ref, around(*rim_rows(ins, 2), ins["skip"].at[0]), own, total)
        for copy in waits:
            copy.wait()

        def store(row, v):
            out[0][row] = v

        finish([x_ref, s_ref], halves, y_ref, bias_ref, bias, None, store)

    w_half = ((TAPS, kd * ring // 2, outs), BF)
    d0, w_dec, w_skip = call(
        {**d_pieces, **rims, "dec": dec_in, "skip": skip, "bias": decoder_bias},
        [((own + 2,) + image, BF), w_half, w_half],
        dec0_body,
        [x_scratch(own + 4)] * 2
        + [y_scratch(own + 2), pltpu.SemaphoreType.DMA((8,))]
        + bias_scratch,
        cost(own + 2, 2),
        {"bias": "hbm"} | {f"p{i}": "any" for i in range(8)},
    )

    handed = {1: ("e0", 2, own + 2), 2: ("e1", 0, own + 4), 3: ("e2", 0, own + 2)}
    results = {f"e{n}": made[n] for n in range(3)}

    def handed_view(ins, t):
        name, at, rows = handed[t]
        return ins[name].at[at : at + rows]

    def skip_body(t, ins, out, scratch):
        x_ref, y_ref = scratch
        lag = 2 * (segments - lax.axis_index("segment")) - 1
        cases = [(lag == 1, [handed_view(ins, t)])]
        plain = lag != 1
        if t == 3:
            cases.append((lag == 3, [handed_view(ins, 1)]))
            plain = plain & (lag != 3)
        cases += around(*rim_rows(ins, 2 + t), ins["skip"].at[t], also=plain)
        fill(x_ref, cases, own, total)
        products(patches(x_ref), [ins["w"]], y_ref)
        for row in range(out[0].shape[0]):
            out[0][row] = combine(y_ref, row, width)

    acc = []
    for t, rows in ((1, own), (2, own + 2), (3, own)):
        used = {handed[t][0], handed[1][0]} if t == 3 else {handed[t][0]}
        acc += call(
            {**rims, **{n: results[n] for n in sorted(used)}, "skip": skip, "w": w_skip},
            [((rows, width, outs), F32)],
            lambda ins, out, scratch, t=t: skip_body(t, ins, out, scratch),
            [x_scratch(rows + 2), y_scratch(rows)],
            cost(rows),
        )

    def dec_body(t, moved, ins, out, scratch):
        x_ref, y_ref, bias_ref, few = scratch
        (bias,) = begin([(ins["bias"], bias_ref)], few)
        last = lax.axis_index("segment") == segments - 1
        cases = [(~last, [ins[m] for m in moved]), (last, [handed_view(ins, t)])]
        fill(x_ref, cases, own, total)
        if t == 3:
            out[0][0] = ins["d0"][1 : 1 + own]
            out[0][1] = ins["d1"][...]
            out[0][2] = ins["d2"][1 : 1 + own]

        def store(row, v):
            if t == 3:
                out[0][3, row] = v
            else:
                out[0][row] = v
            if t == 1 and row < 2:
                out[1][row] = v
            if t == 1 and row >= own - 2:
                out[2][row - own + 2] = v

        finish([x_ref], [ins["w"]], y_ref, bias_ref, bias, ins["acc"], store)

    def dec(t, rows, moved, shapes, more=()):
        arrays = dict(moved)
        name = handed[t][0]
        arrays |= {name: results[name], "w": w_dec, "bias": decoder_bias, "acc": acc[t - 1]}
        arrays |= dict(more)
        return call(
            arrays,
            [(s + image, BF) for s in shapes],
            lambda ins, out, scratch: dec_body(t, list(moved), ins, out, scratch),
            [x_scratch(rows + 2), y_scratch(rows)] + bias_scratch,
            cost(rows),
            {"bias": "hbm"},
        )

    d1, d1_head, d1_last = dec(1, own, {"m": send(d0, down)}, [(own,), (2,), (2,)])
    moved = {
        "before": send(d1_last, down_after),
        "m": send(d1, down),
        "after": send(d1_head, down_before),
    }
    (d2,) = dec(2, own + 2, moved, [(own + 2,)])
    (dec_all,) = dec(3, own, {"m": send(d2, down)}, [(4, own)], {"d0": d0, "d1": d1, "d2": d2})
    shape = (1, 4, 1, own, width, outs)
    return enc_all.reshape(shape), dec_all.reshape(shape)


def solution(mesh):
    return jax.shard_map(
        shards,
        mesh=mesh,
        in_specs=(
            P("segment", None, None, "rows", None),
            P("segment", None),
            P("segment", None, None, "rows", None),
            P("segment", None),
            P("segment", None, "rows", None, None),
            P("segment", None, "rows", None, None),
            P(None, None, "rows", None, None),
            P("segment", None, None, "rows", None, None),
        ),
        out_specs=(
            P("segment", None, None, "rows", None, None),
            P("segment", None, None, "rows", None, None),
        ),
        check_vma=False,
    )
```
